32 devices in a mesh: seq: 16 (over z, y, x), head: 2 (over core).
Axes of the slice: x: 2, y: 2, z: 4, core: 2. Of those that a mesh axis runs over, the one named last changes fastest.
Arguments:
- linear_query: bfloat16 [2048, 8192], P('seq', 'head'), may hold values from -6 to 6
- linear_key: bfloat16 [2048, 8192], P('seq', 'head'), may hold values from -6 to 6
- linear_value: bfloat16 [2048, 8192], P('seq', 'head'), may hold values from -120 to 120
- linear_gate: bfloat16 [2048, 8192], P('seq', 'head'), may hold values from -6 to 6
- log_decay: float32 [64, 2048], P('head', 'seq'), may hold values from -1 to 0
- norm_gain: float32 [8192], P('head'), may hold values from 0.25 to 1.75
- soft_query: bfloat16 [2048, 8192], P('seq', 'head'), may hold values from -6 to 6
- soft_key: bfloat16 [2048, 1024], P('seq', 'head'), may hold values from -6 to 6
- soft_value: bfloat16 [2048, 1024], P('seq', 'head'), may hold values from -6 to 6
- segment_lengths: int32 [4], replicated, may hold values from 1 to 1024, 2048 in all
Outputs:
- linear_mixed: bfloat16 [2048, 8192], P('seq', 'head')
- soft_mixed: bfloat16 [2048, 8192], P('seq', 'head')
The draws below stay inside these ranges and needn't reach their ends.
Inputs may be any that keep to these rules, and one draw needn't show every extreme that they name: `segment_lengths`: the lengths add up to 2048, and the longest is exactly 1024.
All inputs are finite; a program needn't handle non-finite values.
Results may differ from the reference program's by a relative error of at most 0.0036.
Values may be sent and summed in bfloat16 or wider, within the bound.
A program may use at most 128 MiB of HBM per device.

```python
import math
import jax
import jax.numpy as jnp
import numpy as np
from jax import lax

ATTENTION_HEADS = 64
KV_HEADS = 8
HEAD_DIM = 128
FEATURES = 8192
TOK_DEV = 128
REACH = 8
PACKED_TOKENS = 2048
SEG_MOST = 1024
NSEG = 4


def draw_log_decay(key, part):
    divided_random_keys = jax.random.split(key, 6)
    fast_heads = jax.random.randint(divided_random_keys[0], (ATTENTION_HEADS,), 0, 16) < 8
    speed = jnp.exp(jax.random.uniform(divided_random_keys[1], (ATTENTION_HEADS,), minval=math.log(0.6), maxval=math.log(1.6)))
    baseline_speed = jnp.where(fast_heads, -0.075 * speed, -0.5 * speed / PACKED_TOKENS)
    processor_multiplier = jnp.exp(jax.random.uniform(divided_random_keys[2], (ATTENTION_HEADS, PACKED_TOKENS // TOK_DEV), minval=math.log(0.5), maxval=math.log(2.0)))
    processor_multiplier = jnp.repeat(processor_multiplier, TOK_DEV, axis=1)
    jitter_amplitude = jax.random.uniform(divided_random_keys[3], (ATTENTION_HEADS, PACKED_TOKENS), minval=0.5, maxval=1.5)
    spike_locations = jax.random.randint(divided_random_keys[4], (ATTENTION_HEADS, 3), 0, PACKED_TOKENS)
    spike_penalty = jax.random.uniform(divided_random_keys[5], (ATTENTION_HEADS, 3), minval=0.2, maxval=0.4)
    spike_occurrences = (spike_locations[:, :, None] == jnp.arange(PACKED_TOKENS)[None, None, :]).astype(jnp.float32)
    spike_events = jnp.sum(spike_occurrences * jnp.log(1.0 - spike_penalty)[:, :, None], axis=1)
    return (baseline_speed[:, None] * processor_multiplier * jitter_amplitude + spike_events).astype(jnp.float32)


def draw_linear_value(key, part):
    divided_random_keys = jax.random.split(jax.random.fold_in(key, 3), 2)
    head_number = (jnp.arange(FEATURES) // HEAD_DIM).astype(jnp.float32)
    base_rows = jnp.clip(jax.random.normal(divided_random_keys[0], (PACKED_TOKENS, FEATURES)), -6.0, 6.0)
    ramp = 1.0 + head_number / (ATTENTION_HEADS - 1)
    column = jnp.exp(jax.random.uniform(divided_random_keys[1], (FEATURES,), minval=0.0, maxval=math.log(10.0)))
    return (base_rows * (ramp * column)[None, :]).astype(jnp.bfloat16)


def soft_pair(key):
    divided_random_keys = jax.random.split(jax.random.fold_in(key, 7), 2)
    query_shape = (PACKED_TOKENS, ATTENTION_HEADS * HEAD_DIM)
    key_shape = (PACKED_TOKENS, KV_HEADS * HEAD_DIM)
    query_rows = jnp.clip(jax.random.normal(divided_random_keys[0], query_shape), -6.0, 6.0)
    key_rows = jnp.clip(jax.random.normal(divided_random_keys[1], key_shape), -6.0, 6.0)
    return (query_rows, key_rows)


def draw_soft_query(key, part):
    return soft_pair(key)[0].astype(jnp.bfloat16)


def draw_soft_key(key, part):
    return soft_pair(key)[1].astype(jnp.bfloat16)


def block_levels(rng, shape, pieces, smallest, largest):
    loudness, own = 1.0, jax.random.fold_in(rng, 6)
    for position, parts in pieces:
        heights = jnp.exp(jax.random.uniform(jax.random.fold_in(own, position), (parts,), jnp.float32, smallest / len(pieces), largest / len(pieces)))
        loudness = loudness * jnp.repeat(heights, shape[position] // parts).reshape([-1 if axis == position else 1 for axis in range(len(shape))])
    return loudness


def split_up(count, total, reach, lean):
    weights = [(1 << 20) // math.isqrt(rank ** lean) + 1 for rank in range(2, count + 1)]
    rest, holding = total - reach - (count - 1), [1] * (count - 1)
    while rest > 0:
        free = [i for i in range(count - 1) if holding[i] < reach]
        mass, budget = sum([weights[i] for i in free]), rest
        for i in free:
            extra = min(reach - holding[i], max(1, budget * weights[i] // mass), rest)
            holding[i] = holding[i] + extra
            rest = rest - extra
    return np.array([reach] + holding)


def uneven_parts(own_key, count, total, bound, slope):
    if count == 2:
        one = jax.random.randint(own_key, (), max(1, total - bound), min(bound, total - 1) + 1)
        return jnp.stack([one, total - one])
    sizes = jnp.asarray(split_up(count, total, bound, slope), jnp.int32)
    twos = (count - 1) // 2
    giver, sink = sizes[1:1 + 2 * twos:2], sizes[2:2 + 2 * twos:2]
    margin = jnp.minimum(giver - 1, bound - sink)
    passed = jax.random.randint(jax.random.fold_in(own_key, 1), (twos,), 0, 1 << 20) % (margin + 1)
    sizes = sizes.at[1:1 + 2 * twos:2].set(giver - passed).at[2:2 + 2 * twos:2].set(sink + passed)
    return sizes[jax.random.permutation(jax.random.fold_in(own_key, 2), count)]


def scatter_about(rng, dims, width, most, cuts=(), kind=jnp.bfloat16):
    factor_of = block_levels(rng, dims, cuts, -0.22, 0.18) if cuts else 1.0
    values = jax.random.normal(rng, dims, jnp.float32) * width * factor_of
    return jnp.minimum(jnp.maximum(values, -most), most).astype(kind)


def setup_inputs(seed: int = 0) -> dict:
    seeds = jax.random.split(jax.random.key(seed), 11)
    linear_query = scatter_about(seeds[0], (PACKED_TOKENS, FEATURES), 1.0, 6.0, ((0, 16), (1, 2)))
    linear_key = scatter_about(seeds[1], (PACKED_TOKENS, FEATURES), 1.0, 6.0, ((0, 16), (1, 2)))
    linear_value = draw_linear_value(jax.random.fold_in(seeds[10], 71), 0)
    linear_gate = scatter_about(seeds[3], (PACKED_TOKENS, FEATURES), 1.5, 6.0, ((0, 16), (1, 2)))
    log_decay = draw_log_decay(jax.random.fold_in(seeds[10], 71), 0)
    norm_gain = jnp.clip(1.0 + 0.15 * jax.random.normal(seeds[5], (FEATURES,), jnp.float32), 0.25, 1.75)
    soft_query = draw_soft_query(jax.random.fold_in(seeds[10], 71), 0)
    soft_key = draw_soft_key(jax.random.fold_in(seeds[10], 71), 0)
    soft_value = scatter_about(seeds[8], (PACKED_TOKENS, KV_HEADS * HEAD_DIM), 1.0, 6.0, ((0, 16), (1, 2)))
    segment_lengths = uneven_parts(seeds[9], NSEG, PACKED_TOKENS, SEG_MOST, 2).astype(jnp.int32)
    return dict(linear_query=linear_query, linear_key=linear_key, linear_value=linear_value, linear_gate=linear_gate, log_decay=log_decay, norm_gain=norm_gain, soft_query=soft_query, soft_key=soft_key, soft_value=soft_value, segment_lengths=segment_lengths)


norm_eps = 1e-05

def segment_starts(lengths):
    segment_ends = jnp.cumsum(lengths)
    return (segment_ends - lengths).astype(jnp.int32)

def segment_of(starts, positions):
    inside = (starts[None, :] <= positions[:, None]).astype(jnp.int32)
    return (lax.optimization_barrier(jnp.sum(inside, axis=1)) - 1).astype(jnp.int32)

def light_block(carry_state, block):
    act_query, act_key, act_value, decays, segment_ids, previous_id = block
    offsets = jnp.arange(act_query.shape[0], dtype=jnp.int32)
    cumulative = jnp.cumsum(decays, axis=1)
    same_segment = (offsets[:, None] >= offsets[None, :]) & (segment_ids[:, None] == segment_ids[None, :])
    decay_gap = jnp.where(same_segment[None], cumulative[:, :, None] - cumulative[:, None, :], 0.0)
    weights = jnp.where(same_segment[None], jnp.exp(decay_gap), 0.0)
    query_wide = act_query.astype(jnp.float32)
    key_wide = act_key.astype(jnp.float32)
    value_wide = act_value.astype(jnp.float32)
    scores = jnp.einsum('thd,shd->hts', query_wide, key_wide)
    decayed = lax.optimization_barrier((scores * weights).astype(jnp.bfloat16))
    local_part = jnp.einsum('hts,shd->thd', decayed.astype(jnp.float32), value_wide)
    inflow = jnp.where(segment_ids[None, :] == previous_id, jnp.exp(cumulative), 0.0)
    carried = jnp.einsum('thd,hde->the', query_wide, carry_state, precision=lax.Precision.HIGHEST) * jnp.transpose(inflow)[:, :, None]
    last_segment = segment_ids[-1]
    tail_weight = jnp.where(segment_ids[None, :] == last_segment, jnp.exp(cumulative[:, -1:] - cumulative), 0.0)
    tail_key = lax.optimization_barrier((key_wide * jnp.transpose(tail_weight)[:, :, None]).astype(jnp.bfloat16))
    fresh_state = jnp.einsum('thd,the->hde', tail_key.astype(jnp.float32), value_wide)
    factor = jnp.where(last_segment == previous_id, jnp.exp(cumulative[:, -1]), 0.0)
    carry_state = factor[:, None, None] * carry_state + fresh_state
    return (carry_state, local_part + carried)

def attend_group(group_query, group_keys, group_values, visible):
    score_scale = 1.0 / math.sqrt(HEAD_DIM)
    scores = jnp.einsum('gtd,sd->gts', group_query, group_keys) * score_scale
    scores = jnp.where(visible[None], scores, -jnp.inf)
    row_top = lax.optimization_barrier(jnp.max(scores, axis=2, keepdims=True))
    weight = jnp.exp(scores - row_top)
    row_total = lax.optimization_barrier(jnp.sum(weight, axis=2, keepdims=True))
    weight_bf = lax.optimization_barrier(weight.astype(jnp.bfloat16))
    mixed_rows = jnp.einsum('gts,sd->gtd', weight_bf.astype(jnp.float32), group_values)
    return (mixed_rows / row_total).astype(jnp.bfloat16)

def reference(linear_query, linear_key, linear_value, linear_gate, log_decay, norm_gain, soft_query, soft_key, soft_value, segment_lengths):
    starts = segment_starts(segment_lengths)
    positions = jnp.arange(PACKED_TOKENS, dtype=jnp.int32)
    segment_ids = segment_of(starts, positions)
    blocks = PACKED_TOKENS // TOK_DEV
    block_firsts = jnp.arange(blocks, dtype=jnp.int32) * TOK_DEV
    previous_ids = segment_of(starts, (block_firsts - 1).astype(jnp.int32))

    def activate(raw):
        return lax.optimization_barrier(jax.nn.silu(raw.astype(jnp.float32)).astype(jnp.bfloat16)).reshape(blocks, TOK_DEV, ATTENTION_HEADS, HEAD_DIM)
    decays = jnp.transpose(log_decay.reshape(ATTENTION_HEADS, blocks, TOK_DEV), (1, 0, 2))
    carry_state = jnp.zeros((ATTENTION_HEADS, HEAD_DIM, HEAD_DIM), jnp.float32)
    carry_state, block_outputs = lax.scan(light_block, carry_state, (activate(linear_query), activate(linear_key), activate(linear_value), decays, segment_ids.reshape(blocks, TOK_DEV), previous_ids))
    linear_out = block_outputs.reshape(PACKED_TOKENS, FEATURES)
    mean_square = lax.optimization_barrier(jnp.mean(linear_out * linear_out, axis=1, keepdims=True))
    gate_value = jax.nn.sigmoid(linear_gate.astype(jnp.float32))
    linear_mixed = (linear_out * lax.rsqrt(mean_square + norm_eps) * norm_gain[None, :] * gate_value).astype(jnp.bfloat16)
    span_rows = (REACH + 1) * TOK_DEV
    group_size = ATTENTION_HEADS // KV_HEADS
    zero_rows = jnp.zeros((REACH * TOK_DEV, KV_HEADS * HEAD_DIM), soft_key.dtype)
    key_pad = jnp.concatenate([zero_rows, soft_key], axis=0)
    value_pad = jnp.concatenate([zero_rows, soft_value], axis=0)

    def soft_block(block_index):
        first_row = (block_index * TOK_DEV).astype(jnp.int32)
        query_rows = first_row + jnp.arange(TOK_DEV, dtype=jnp.int32)
        key_positions = first_row - REACH * TOK_DEV + jnp.arange(span_rows, dtype=jnp.int32)
        visible = (key_positions[None, :] <= query_rows[:, None]) & (segment_of(starts, key_positions)[None, :] == segment_of(starts, query_rows)[:, None])
        block_query = lax.dynamic_slice_in_dim(soft_query, first_row, TOK_DEV, 0).astype(jnp.float32)
        block_query = jnp.transpose(block_query.reshape(TOK_DEV, KV_HEADS, group_size, HEAD_DIM), (1, 2, 0, 3))
        block_keys = lax.dynamic_slice_in_dim(key_pad, first_row, span_rows, 0).astype(jnp.float32)
        block_keys = jnp.transpose(block_keys.reshape(span_rows, KV_HEADS, HEAD_DIM), (1, 0, 2))
        block_values = lax.dynamic_slice_in_dim(value_pad, first_row, span_rows, 0).astype(jnp.float32)
        block_values = jnp.transpose(block_values.reshape(span_rows, KV_HEADS, HEAD_DIM), (1, 0, 2))

        def per_group(group_item):
            return attend_group(group_item[0], group_item[1], group_item[2], visible)
        attended = lax.map(per_group, (block_query, block_keys, block_values))
        return jnp.transpose(attended, (2, 0, 1, 3)).reshape(TOK_DEV, FEATURES)
    soft_mixed = lax.map(soft_block, jnp.arange(blocks, dtype=jnp.int32)).reshape(PACKED_TOKENS, FEATURES)
    return (linear_mixed, soft_mixed)
```

```python
import functools
import math

import jax
import jax.numpy as jnp
from jax import lax
from jax.experimental import pallas as pl
from jax.experimental.pallas import tpu as pltpu
from jax.sharding import PartitionSpec as P

ATTENTION_HEADS = 64
KV_HEADS = 8
D = 128
REACH = 8
PLANE = 4
NORM_EPS = 1e-05
MESH = pl.DeviceIdType.MESH
BF16 = jnp.bfloat16
F32 = jnp.float32
HIDE = -1e30


def sigmoid(x):
    return 0.5 * jnp.tanh(0.5 * x) + 0.5


def silu(raw):
    x = raw.astype(F32)
    return (x * sigmoid(x)).astype(BF16)


def head_cols(h):
    return pl.ds(pl.multiple_of(h * D, D), D)


def kernel(
    planes,
    head_size,
    lq,
    lk,
    lv,
    lg,
    ld,
    gain,
    sq,
    sk,
    sv,
    lens,
    lin_out,
    soft_out,
    qact,
    kact,
    vact,
    acc,
    kwin,
    vwin,
    fresh,
    fac,
    got,
    got_fac,
    tot,
    tot_fac,
    t1,
    t2,
    f1,
    ibuf,
    inc,
    cumrow,
    near,
    wide,
    sqsum,
    sqgot,
    kv_send,
    kv_recv,
    fr_send,
    fr_recv,
    t_send,
    t_recv,
    i_send,
    i_recv,
    s_send,
    s_recv,
):
    rows = lq.shape[0]
    heads = lq.shape[1] // D
    owned = heads // PLANE
    group = ATTENTION_HEADS // KV_HEADS
    span = (REACH + 1) * rows
    me = lax.axis_index("seq")
    hd = lax.axis_index("head")
    z = me // PLANE
    o = me % PLANE

    def dev(zz, oo):
        return (zz * PLANE + oo, hd)

    barrier = pltpu.get_barrier_semaphore()

    def greet(device):
        pl.semaphore_signal(barrier, inc=1, device_id=device, device_id_type=MESH)

    for p in range(PLANE):

        @pl.when(p != o)
        def _():
            greet(dev(z, p))

    for step in (1, 2):

        @pl.when(z + step < planes)
        def _():
            greet(dev(z + step, o))

        @pl.when(z - step >= 0)
        def _():
            greet(dev(z - step, o))

    for hp in range(head_size):

        @pl.when(hp != hd)
        def _():
            greet((me, hp))

    count = PLANE - 1 + head_size - 1
    for step in (1, 2):
        count = count + jnp.where(z + step < planes, 1, 0) + jnp.where(z - step >= 0, 1, 0)
    pl.semaphore_wait(barrier, count)

    def kv_pair(k_src, v_src, slot, which, device):
        return (
            pltpu.make_async_remote_copy(
                src_ref=k_src,
                dst_ref=kwin.at[slot],
                send_sem=kv_send.at[0, which],
                recv_sem=kv_recv.at[0, slot],
                device_id=device,
                device_id_type=MESH,
            ),
            pltpu.make_async_remote_copy(
                src_ref=v_src,
                dst_ref=vwin.at[slot],
                send_sem=kv_send.at[1, which],
                recv_sem=kv_recv.at[1, slot],
                device_id=device,
                device_id_type=MESH,
            ),
        )

    def kv_up(step):
        return kv_pair(sk, sv, REACH - PLANE * step, 3 * PLANE + step - 1, dev(z + step, o))

    def kv_own(p):
        return kv_pair(sk, sv, jnp.clip(REACH - (p - o), 0, REACH), p, dev(z, p))

    def kv_relay(step, p):
        base = REACH - PLANE * step
        return kv_pair(
            kwin.at[base],
            vwin.at[base],
            jnp.clip(base - (p - o), 0, REACH),
            PLANE * step + p,
            dev(z, p),
        )

    def start(pair):
        for c in pair:
            c.start()

    def wait_recv(pair):
        for c in pair:
            c.wait_recv()

    def wait_send(pair):
        for c in pair:
            c.wait_send()

    for step in (1, 2):

        @pl.when(z + step < planes)
        def _():
            start(kv_up(step))

    for p in range(PLANE):

        @pl.when(p > o)
        def _():
            start(kv_own(p))

    kwin[REACH] = sk[...]
    vwin[REACH] = sv[...]
    for slot in range(REACH):

        @pl.when(me - (REACH - slot) < 0)
        def _():
            kwin[slot] = jnp.zeros(kwin.shape[1:], BF16)
            vwin[slot] = jnp.zeros(vwin.shape[1:], BF16)

    nseg = lens.shape[0]
    first = me * rows
    starts = []
    run = jnp.int32(0)
    for i in range(nseg):
        starts.append(run)
        run = run + lens[i]

    def start_of(position):
        best = jnp.zeros_like(position)
        for s in starts:
            best = jnp.where(s <= position, s, best)
        return best

    t_id = lax.broadcasted_iota(jnp.int32, (rows, rows), 0)
    s_id = lax.broadcasted_iota(jnp.int32, (rows, rows), 1)
    own_start = start_of(first + t_id)
    near[...] = jnp.where((s_id <= t_id) & (first + s_id >= own_start), 0.0, HIDE)
    for j in range(REACH + 1):
        key_pos = first + (j - REACH) * rows + s_id
        wide[:, j * rows : (j + 1) * rows] = jnp.where(
            (key_pos <= first + t_id) & (key_pos >= own_start), 0.0, HIDE
        )
    last_start = start_of(first + rows - 1)
    t_col = lax.broadcasted_iota(jnp.int32, (rows, 1), 0)
    tail_on = first + t_col >= last_start
    in_on = start_of(first + t_col) <= first - 1
    through = last_start <= first - 1
    upto = s_id <= t_id
    cumrow[...] = jnp.dot(
        ld[...],
        (t_id <= s_id).astype(F32),
        precision=lax.Precision.HIGHEST,
        preferred_element_type=F32,
    )

    def fr_pair(c, source):
        return (
            pltpu.make_async_remote_copy(
                src_ref=fresh.at[c],
                dst_ref=got.at[source],
                send_sem=fr_send.at[0, c],
                recv_sem=fr_recv.at[0, source],
                device_id=dev(z, c),
                device_id_type=MESH,
            ),
            pltpu.make_async_remote_copy(
                src_ref=fac.at[c],
                dst_ref=got_fac.at[source],
                send_sem=fr_send.at[1, c],
                recv_sem=fr_recv.at[1, source],
                device_id=dev(z, c),
                device_id_type=MESH,
            ),
        )

    def chunk(j, carry):
        c = (o + 1 + j) % PLANE

        def one(hh, carry):
            h = c * owned + hh
            cols = head_cols(h)
            k = silu(lk[:, cols])
            v = silu(lv[:, cols])
            kact[:, cols] = k
            vact[:, cols] = v
            decay = ld[pl.ds(h, 1), :]
            later = jnp.sum(jnp.where(upto, 0.0, decay), axis=1, keepdims=True)
            weight = jnp.where(tail_on, jnp.exp(later), 0.0)
            tail = (k.astype(F32) * weight).astype(BF16)
            state = lax.dot_general(
                tail, v, (((0,), (0,)), ((), ())), preferred_element_type=F32
            )
            fresh[c, hh] = state.astype(BF16)
            whole = jnp.sum(decay, axis=1, keepdims=True)
            fac[c, hh] = jnp.broadcast_to(jnp.where(through, jnp.exp(whole), 0.0), (8, D))
            return carry

        lax.fori_loop(0, owned, one, 0, unroll=2)

        @pl.when(j < PLANE - 1)
        def _():
            start(fr_pair(c, o))

        return carry

    lax.fori_loop(0, PLANE, chunk, 0)
    got[o] = fresh[o]
    got_fac[o] = fac[o]

    def relay(step):
        @pl.when(z >= step)
        def _():
            wait_recv(kv_pair(sk, sv, REACH - PLANE * step, 0, dev(z, o)))
            for p in range(PLANE):

                @pl.when((p != o) if step == 1 else (p < o))
                def _():
                    start(kv_relay(step, p))

    def local(h, carry):
        cols = head_cols(h)
        q = silu(lq[:, cols])
        qact[:, cols] = q
        decay = ld[pl.ds(h, 1), :]
        col = jnp.sum(jnp.where(upto, decay, 0.0), axis=1, keepdims=True)
        weight = jnp.exp(col - cumrow[pl.ds(h, 1), :] + near[...])
        score = lax.dot_general(
            q, kact[:, cols], (((1,), (1,)), ((), ())), preferred_element_type=F32
        )
        acc[:, cols] = jnp.dot(
            (score * weight).astype(BF16), vact[:, cols], preferred_element_type=F32
        )
        return carry

    lax.fori_loop(0, heads, local, 0, unroll=2)
    relay(1)

    for i in range(PLANE):

        @pl.when(i != o)
        def _():
            wait_recv(fr_pair(o, i))

    def total(hh, carry):
        value = got[0, hh].astype(F32)
        factor = got_fac[0, hh]
        for i in range(1, PLANE):
            f = got_fac[i, hh]
            value = value * f[0:1, :] + got[i, hh].astype(F32)
            factor = factor * f
        tot[hh] = value.astype(BF16)
        tot_fac[hh] = factor
        return carry

    lax.fori_loop(0, owned, total, 0)

    def up_copy(src, dst, which, step):
        return pltpu.make_async_remote_copy(
            src_ref=src,
            dst_ref=dst,
            send_sem=t_send.at[which],
            recv_sem=t_recv.at[which],
            device_id=dev(z + step, o),
            device_id_type=MESH,
        )

    ups = (up_copy(tot, t1, 0, 1), up_copy(tot_fac, f1, 1, 1), up_copy(tot, t2, 2, 2))

    @pl.when(z + 1 < planes)
    def _():
        ups[0].start()
        ups[1].start()

    @pl.when(z + 2 < planes)
    def _():
        ups[2].start()

    relay(2)

    @pl.when(z < 1)
    def _():
        t1[...] = jnp.zeros_like(t1)
        f1[...] = jnp.zeros_like(f1)

    @pl.when(z < 2)
    def _():
        t2[...] = jnp.zeros_like(t2)

    for slot in (1, 2, 3, 5, 6, 7):

        @pl.when(me - (REACH - slot) >= 0)
        def _():
            wait_recv(kv_pair(sk, sv, slot, 0, dev(z, o)))

    score_scale = math.log2(math.e) / math.sqrt(D)

    def attend(i, carry):
        kv_cols = head_cols(i // (group // 2))
        keys = kwin[:, :, kv_cols].reshape(span, D)
        values = vwin[:, :, kv_cols].reshape(span, D)
        ca = head_cols(2 * i)
        cb = head_cols(2 * i + 1)
        query = jnp.concatenate([sq[:, ca], sq[:, cb]], axis=0)
        score = lax.dot_general(
            query, keys, (((1,), (1,)), ((), ())), preferred_element_type=F32
        )
        score = (score * score_scale).reshape(2, rows, span) + wide[...][None]
        score = score.reshape(2 * rows, span)
        top = jnp.max(score, axis=1, keepdims=True)
        weight = jnp.exp2(score - top)
        whole = jnp.sum(weight, axis=1, keepdims=True)
        mixed = jnp.dot(weight.astype(BF16), values, preferred_element_type=F32) / whole
        soft_out[:, ca] = mixed[:rows].astype(BF16)
        soft_out[:, cb] = mixed[rows:].astype(BF16)
        return carry

    pairs = heads // 2
    lax.fori_loop(0, pairs // 2, attend, 0)

    @pl.when(z >= 1)
    def _():
        ups[0].wait_recv()
        ups[1].wait_recv()

    @pl.when(z >= 2)
    def _():
        ups[2].wait_recv()

    def enter(hh, carry):
        value = t1[hh].astype(F32) + f1[hh][0:1, :] * t2[hh].astype(F32)
        for p in range(PLANE):
            ibuf[p, hh] = value.astype(BF16)
            if p < PLANE - 1:
                value = got_fac[p, hh][0:1, :] * value + got[p, hh].astype(F32)
        return carry

    lax.fori_loop(0, owned, enter, 0)

    def in_copy(p, source):
        return pltpu.make_async_remote_copy(
            src_ref=ibuf.at[p],
            dst_ref=inc.at[source],
            send_sem=i_send.at[p],
            recv_sem=i_recv.at[source],
            device_id=dev(z, p),
            device_id_type=MESH,
        )

    for p in range(PLANE):

        @pl.when(p != o)
        def _():
            in_copy(p, o).start()

    inc[o] = ibuf[o]
    lax.fori_loop(pairs // 2, pairs, attend, 0)

    for i in range(PLANE):

        @pl.when(i != o)
        def _():
            in_copy(i, i).wait_recv()

    sqsum[...] = jnp.zeros_like(sqsum)

    def carried(h, carry):
        cols = head_cols(h)
        decay = ld[pl.ds(h, 1), :]
        col = jnp.sum(jnp.where(upto, decay, 0.0), axis=1, keepdims=True)
        inflow = jnp.where(in_on, jnp.exp(col), 0.0)
        flow = jnp.dot(
            qact[:, cols], inc[h // owned, h % owned], preferred_element_type=F32
        )
        out = acc[:, cols] + flow * inflow
        acc[:, cols] = out
        sqsum[...] += out * out
        return carry

    lax.fori_loop(0, heads, carried, 0, unroll=2)

    def sq_copy(hp, source):
        return pltpu.make_async_remote_copy(
            src_ref=sqsum,
            dst_ref=sqgot.at[source],
            send_sem=s_send.at[hp],
            recv_sem=s_recv.at[source],
            device_id=(me, hp),
            device_id_type=MESH,
        )

    for hp in range(head_size):

        @pl.when(hp != hd)
        def _():
            sq_copy(hp, hd).start()

    sqgot[hd] = sqsum[...]
    for hp in range(head_size):

        @pl.when(hp != hd)
        def _():
            sq_copy(hp, hp).wait_recv()

    squares = sqgot[0]
    for hp in range(1, head_size):
        squares = squares + sqgot[hp]
    features = head_size * heads * D
    norm = lax.rsqrt(jnp.sum(squares, axis=1, keepdims=True) / features + NORM_EPS)

    def finish(h, carry):
        cols = head_cols(h)
        gate = sigmoid(lg[:, cols].astype(F32))
        lin_out[:, cols] = (acc[:, cols] * norm * gain[:, cols] * gate).astype(BF16)
        return carry

    lax.fori_loop(0, heads, finish, 0, unroll=2)

    for step in (1, 2):

        @pl.when(z + step < planes)
        def _():
            wait_send(kv_up(step))

    for p in range(PLANE):

        @pl.when(p > o)
        def _():
            wait_send(kv_own(p))

        @pl.when((p != o) & (z >= 1))
        def _():
            wait_send(kv_relay(1, p))

        @pl.when((p < o) & (z >= 2))
        def _():
            wait_send(kv_relay(2, p))

        @pl.when(p != o)
        def _():
            wait_send(fr_pair(p, o))
            in_copy(p, o).wait_send()

    @pl.when(z + 1 < planes)
    def _():
        ups[0].wait_send()
        ups[1].wait_send()

    @pl.when(z + 2 < planes)
    def _():
        ups[2].wait_send()

    for hp in range(head_size):

        @pl.when(hp != hd)
        def _():
            sq_copy(hp, hd).wait_send()


def on_device(planes, head_size, lq, lk, lv, lg, ld, gain, sq, sk, sv, lens):
    rows, width = lq.shape
    heads = width // D
    owned = heads // PLANE
    kv_width = sk.shape[1]
    vmem = pl.BlockSpec(memory_space=pltpu.VMEM)
    dma = pltpu.SemaphoreType.DMA
    states = (owned, D, D)
    factors = (owned, 8, D)
    return pl.pallas_call(
        functools.partial(kernel, planes, head_size),
        out_shape=(
            jax.ShapeDtypeStruct((rows, width), BF16),
            jax.ShapeDtypeStruct((rows, width), BF16),
        ),
        in_specs=[vmem] * 9 + [pl.BlockSpec(memory_space=pltpu.SMEM)],
        out_specs=(vmem, vmem),
        scratch_shapes=[
            pltpu.VMEM((rows, width), BF16),
            pltpu.VMEM((rows, width), BF16),
            pltpu.VMEM((rows, width), BF16),
            pltpu.VMEM((rows, width), F32),
            pltpu.VMEM((REACH + 1, rows, kv_width), BF16),
            pltpu.VMEM((REACH + 1, rows, kv_width), BF16),
            pltpu.VMEM((PLANE,) + states, BF16),
            pltpu.VMEM((PLANE,) + factors, F32),
            pltpu.VMEM((PLANE,) + states, BF16),
            pltpu.VMEM((PLANE,) + factors, F32),
            pltpu.VMEM(states, BF16),
            pltpu.VMEM(factors, F32),
            pltpu.VMEM(states, BF16),
            pltpu.VMEM(states, BF16),
            pltpu.VMEM(factors, F32),
            pltpu.VMEM((PLANE,) + states, BF16),
            pltpu.VMEM((PLANE,) + states, BF16),
            pltpu.VMEM((heads, rows), F32),
            pltpu.VMEM((rows, rows), F32),
            pltpu.VMEM((rows, (REACH + 1) * rows), F32),
            pltpu.VMEM((rows, D), F32),
            pltpu.VMEM((head_size, rows, D), F32),
            dma((2, 3 * PLANE + 2)),
            dma((2, REACH + 1)),
            dma((2, PLANE)),
            dma((2, PLANE)),
            dma((3,)),
            dma((3,)),
            dma((PLANE,)),
            dma((PLANE,)),
            dma((head_size,)),
            dma((head_size,)),
        ],
        compiler_params=pltpu.CompilerParams(
            collective_id=0, has_side_effects=True, vmem_limit_bytes=56 << 20
        ),
    )(lq, lk, lv, lg, ld, gain.reshape(1, width), sq, sk, sv, lens)


def solution(mesh):
    tokens = P("seq", "head")
    body = functools.partial(on_device, mesh.shape["seq"] // PLANE, mesh.shape["head"])
    return jax.shard_map(
        body,
        mesh=mesh,
        in_specs=(tokens,) * 4 + (P("head", "seq"), P("head")) + (tokens,) * 3 + (P(),),
        out_specs=(tokens, tokens),
        check_vma=False,
    )
```

```python
import functools
import math

import jax
import jax.numpy as jnp
from jax import lax
from jax.experimental import pallas as pl
from jax.experimental.pallas import tpu as pltpu
from jax.sharding import PartitionSpec as P

ATTENTION_HEADS = 64
KV_HEADS = 8
D = 128
REACH = 8
PLANE = 4
NORM_EPS = 1e-05
MESH = pl.DeviceIdType.MESH
BF16 = jnp.bfloat16
F32 = jnp.float32
HIDE = -1e30


def sigmoid(x):
    return 0.5 * jnp.tanh(0.5 * x) + 0.5


def silu(raw):
    x = raw.astype(F32)
    return (x * sigmoid(x)).astype(BF16)


def head_cols(h):
    return pl.ds(pl.multiple_of(h * D, D), D)


def kernel(
    planes,
    head_size,
    lq,
    lk,
    lv,
    lg,
    ld,
    gain,
    sq,
    sk,
    sv,
    lens,
    lin_out,
    soft_out,
    qact,
    kact,
    vact,
    acc,
    kwin,
    vwin,
    fresh,
    fac,
    got,
    got_fac,
    tot,
    tot_fac,
    t1,
    t2,
    f1,
    ibuf,
    inc,
    cumrow,
    near,
    wide,
    sqsum,
    sqgot,
    kv_send,
    kv_recv,
    fr_send,
    fr_recv,
    t_send,
    t_recv,
    i_send,
    i_recv,
    s_send,
    s_recv,
):
    rows = lq.shape[0]
    heads = lq.shape[1] // D
    owned = heads // PLANE
    group = ATTENTION_HEADS // KV_HEADS
    span = (REACH + 1) * rows
    me = lax.axis_index("seq")
    hd = lax.axis_index("head")
    z = me // PLANE
    o = me % PLANE

    def dev(zz, oo):
        return (zz * PLANE + oo, hd)

    barrier = pltpu.get_barrier_semaphore()

    def greet(device):
        pl.semaphore_signal(barrier, inc=1, device_id=device, device_id_type=MESH)

    for p in range(PLANE):

        @pl.when(p != o)
        def _():
            greet(dev(z, p))

    @pl.when(z + 1 < planes)
    def _():
        greet(dev(z + 1, o))

    @pl.when(z >= 1)
    def _():
        greet(dev(z - 1, o))

    for hp in range(head_size):

        @pl.when(hp != hd)
        def _():
            greet((me, hp))

    count = PLANE - 1 + head_size - 1
    count = count + jnp.where(z + 1 < planes, 1, 0) + jnp.where(z >= 1, 1, 0)
    pl.semaphore_wait(barrier, count)

    kv_heads = sk.shape[1] // D
    parts = math.gcd(4, kv_heads)
    part_cols = kv_heads // parts * D
    early = min(1, parts)

    def kv_pair(part, k_src, v_src, slot, which, device):
        cols = pl.ds(part * part_cols, part_cols)
        return (
            pltpu.make_async_remote_copy(
                src_ref=k_src.at[:, cols],
                dst_ref=kwin.at[slot, :, cols],
                send_sem=kv_send.at[0, part, which],
                recv_sem=kv_recv.at[0, part, slot],
                device_id=device,
                device_id_type=MESH,
            ),
            pltpu.make_async_remote_copy(
                src_ref=v_src.at[:, cols],
                dst_ref=vwin.at[slot, :, cols],
                send_sem=kv_send.at[1, part, which],
                recv_sem=kv_recv.at[1, part, slot],
                device_id=device,
                device_id_type=MESH,
            ),
        )

    far = REACH - PLANE

    def kv_up(part):
        return kv_pair(part, sk, sv, far, 3 * PLANE, dev(z + 1, o))

    def kv_up_again(part):
        return kv_pair(part, kwin.at[far], vwin.at[far], 0, 3 * PLANE + 1, dev(z + 1, o))

    def kv_own(part, p):
        return kv_pair(part, sk, sv, jnp.clip(REACH - (p - o), 0, REACH), p, dev(z, p))

    def kv_relay(part, step, p):
        base = REACH - PLANE * step
        return kv_pair(
            part,
            kwin.at[base],
            vwin.at[base],
            jnp.clip(base - (p - o), 0, REACH),
            PLANE * step + p,
            dev(z, p),
        )

    def kv_got(part, slot):
        wait_recv(kv_pair(part, sk, sv, slot, 0, dev(z, (o + 1) % PLANE)))

    def start(pair):
        for c in pair:
            c.start()

    def wait_recv(pair):
        for c in pair:
            c.wait_recv()

    def wait_send(pair):
        for c in pair:
            c.wait_send()

    def own_plane(part):
        for p in range(PLANE):

            @pl.when(p > o)
            def _():
                start(kv_own(part, p))

    for part in range(parts):

        @pl.when(z + 1 < planes)
        def _():
            start(kv_up(part))

        if part < early:
            own_plane(part)

    kwin[REACH] = sk[...]
    vwin[REACH] = sv[...]
    for slot in range(REACH):

        @pl.when(me - (REACH - slot) < 0)
        def _():
            kwin[slot] = jnp.zeros(kwin.shape[1:], BF16)
            vwin[slot] = jnp.zeros(vwin.shape[1:], BF16)

    nseg = lens.shape[0]
    first = me * rows
    starts = []
    run = jnp.int32(0)
    for i in range(nseg):
        starts.append(run)
        run = run + lens[i]

    def start_of(position):
        best = jnp.zeros_like(position)
        for s in starts:
            best = jnp.where(s <= position, s, best)
        return best

    t_id = lax.broadcasted_iota(jnp.int32, (rows, rows), 0)
    s_id = lax.broadcasted_iota(jnp.int32, (rows, rows), 1)
    own_start = start_of(first + t_id)
    near[...] = jnp.where((s_id <= t_id) & (first + s_id >= own_start), 0.0, HIDE)
    for j in range(REACH + 1):
        key_pos = first + (j - REACH) * rows + s_id
        wide[:, j * rows : (j + 1) * rows] = jnp.where(
            (key_pos <= first + t_id) & (key_pos >= own_start), 0.0, HIDE
        )
    last_start = start_of(first + rows - 1)
    t_col = lax.broadcasted_iota(jnp.int32, (rows, 1), 0)
    tail_on = first + t_col >= last_start
    in_on = start_of(first + t_col) <= first - 1
    through = last_start <= first - 1
    upto = s_id <= t_id
    cumrow[...] = jnp.dot(
        ld[...],
        (t_id <= s_id).astype(F32),
        precision=lax.Precision.HIGHEST,
        preferred_element_type=F32,
    )

    def fr_pair(c, source):
        return (
            pltpu.make_async_remote_copy(
                src_ref=fresh.at[c],
                dst_ref=got.at[source],
                send_sem=fr_send.at[0, c],
                recv_sem=fr_recv.at[0, source],
                device_id=dev(z, c),
                device_id_type=MESH,
            ),
            pltpu.make_async_remote_copy(
                src_ref=fac.at[c],
                dst_ref=got_fac.at[source],
                send_sem=fr_send.at[1, c],
                recv_sem=fr_recv.at[1, source],
                device_id=dev(z, c),
                device_id_type=MESH,
            ),
        )

    def chunk(j, carry):
        c = (o + 1 + j) % PLANE

        def one(hh, carry):
            h = c * owned + hh
            cols = head_cols(h)
            k = silu(lk[:, cols])
            v = silu(lv[:, cols])
            kact[:, cols] = k
            vact[:, cols] = v
            decay = ld[pl.ds(h, 1), :]
            later = jnp.sum(jnp.where(upto, 0.0, decay), axis=1, keepdims=True)
            weight = jnp.where(tail_on, jnp.exp(later), 0.0)
            tail = (k.astype(F32) * weight).astype(BF16)
            state = lax.dot_general(
                tail, v, (((0,), (0,)), ((), ())), preferred_element_type=F32
            )
            fresh[c, hh] = state.astype(BF16)
            whole = jnp.sum(decay, axis=1, keepdims=True)
            fac[c, hh] = jnp.broadcast_to(jnp.where(through, jnp.exp(whole), 0.0), (8, D))
            return carry

        lax.fori_loop(0, owned, one, 0, unroll=2)

        @pl.when(j < PLANE - 1)
        def _():
            start(fr_pair(c, o))

        return carry

    lax.fori_loop(0, PLANE, chunk, 0)
    got[o] = fresh[o]
    got_fac[o] = fac[o]

    @pl.when(z >= 1)
    def _():
        for part in range(parts):
            kv_got(part, far)

            @pl.when(z + 1 < planes)
            def _():
                start(kv_up_again(part))

    def relay(part, step):
        @pl.when(z >= step)
        def _():
            if step == 2:
                kv_got(part, 0)
            for p in range(PLANE):

                @pl.when((p != o) if step == 1 else (p < o))
                def _():
                    start(kv_relay(part, step, p))

    for part in range(early):
        relay(part, 1)

    def local(h, carry):
        cols = head_cols(h)
        q = silu(lq[:, cols])
        qact[:, cols] = q
        decay = ld[pl.ds(h, 1), :]
        col = jnp.sum(jnp.where(upto, decay, 0.0), axis=1, keepdims=True)
        weight = jnp.exp(col - cumrow[pl.ds(h, 1), :] + near[...])
        score = lax.dot_general(
            q, kact[:, cols], (((1,), (1,)), ((), ())), preferred_element_type=F32
        )
        acc[:, cols] = jnp.dot(
            (score * weight).astype(BF16), vact[:, cols], preferred_element_type=F32
        )
        return carry

    lax.fori_loop(0, heads, local, 0, unroll=2)

    for i in range(PLANE):

        @pl.when(i != o)
        def _():
            wait_recv(fr_pair(o, i))

    def total(hh, carry):
        value = got[0, hh].astype(F32)
        factor = got_fac[0, hh]
        for i in range(1, PLANE):
            f = got_fac[i, hh]
            value = value * f[0:1, :] + got[i, hh].astype(F32)
            factor = factor * f
        tot[hh] = value.astype(BF16)
        tot_fac[hh] = factor
        return carry

    lax.fori_loop(0, owned, total, 0)

    def up_copy(src, dst, which):
        return pltpu.make_async_remote_copy(
            src_ref=src,
            dst_ref=dst,
            send_sem=t_send.at[which],
            recv_sem=t_recv.at[which],
            device_id=dev(z + 1, o),
            device_id_type=MESH,
        )

    ups = (up_copy(tot, t1, 0), up_copy(tot_fac, f1, 1), up_copy(t1, t2, 2))

    @pl.when(z + 1 < planes)
    def _():
        ups[0].start()
        ups[1].start()

    for part in range(early):
        relay(part, 2)
    for part in range(early, parts):
        own_plane(part)
        relay(part, 1)
        relay(part, 2)

    @pl.when(z < 1)
    def _():
        t1[...] = jnp.zeros_like(t1)
        f1[...] = jnp.zeros_like(f1)

    @pl.when(z < 2)
    def _():
        t2[...] = jnp.zeros_like(t2)

    @pl.when(z >= 1)
    def _():
        ups[0].wait_recv()
        ups[1].wait_recv()

        @pl.when(z + 1 < planes)
        def _():
            ups[2].start()

    def kv_here(part):
        for slot in (1, 2, 3, 5, 6, 7):

            @pl.when(me - (REACH - slot) >= 0)
            def _():
                kv_got(part, slot)

    score_scale = math.log2(math.e) / math.sqrt(D)

    def attend(i, carry):
        kv_cols = head_cols(i // (group // 2))
        keys = kwin[:, :, kv_cols].reshape(span, D)
        values = vwin[:, :, kv_cols].reshape(span, D)
        ca = head_cols(2 * i)
        cb = head_cols(2 * i + 1)
        query = jnp.concatenate([sq[:, ca], sq[:, cb]], axis=0)
        score = lax.dot_general(
            query, keys, (((1,), (1,)), ((), ())), preferred_element_type=F32
        )
        score = (score * score_scale).reshape(2, rows, span) + wide[...][None]
        score = score.reshape(2 * rows, span)
        top = jnp.max(score, axis=1, keepdims=True)
        weight = jnp.exp2(score - top)
        whole = jnp.sum(weight, axis=1, keepdims=True)
        mixed = jnp.dot(weight.astype(BF16), values, preferred_element_type=F32) / whole
        soft_out[:, ca] = mixed[:rows].astype(BF16)
        soft_out[:, cb] = mixed[rows:].astype(BF16)
        return carry

    pairs = heads // 2

    def soften(part):
        kv_here(part)
        lax.fori_loop(part * pairs // parts, (part + 1) * pairs // parts, attend, 0)

    for part in range(min(1, parts)):
        soften(part)

    @pl.when(z >= 2)
    def _():
        ups[2].wait_recv()

    def enter(hh, carry):
        value = t1[hh].astype(F32) + f1[hh][0:1, :] * t2[hh].astype(F32)
        for p in range(PLANE):
            ibuf[p, hh] = value.astype(BF16)
            if p < PLANE - 1:
                value = got_fac[p, hh][0:1, :] * value + got[p, hh].astype(F32)
        return carry

    lax.fori_loop(0, owned, enter, 0)

    def in_copy(p, source):
        return pltpu.make_async_remote_copy(
            src_ref=ibuf.at[p],
            dst_ref=inc.at[source],
            send_sem=i_send.at[p],
            recv_sem=i_recv.at[source],
            device_id=dev(z, p),
            device_id_type=MESH,
        )

    for p in range(PLANE):

        @pl.when(p != o)
        def _():
            in_copy(p, o).start()

    inc[o] = ibuf[o]
    for part in range(min(1, parts), parts):
        soften(part)

    for i in range(PLANE):

        @pl.when(i != o)
        def _():
            in_copy(i, i).wait_recv()

    sqsum[...] = jnp.zeros_like(sqsum)

    def carried(h, carry):
        cols = head_cols(h)
        decay = ld[pl.ds(h, 1), :]
        col = jnp.sum(jnp.where(upto, decay, 0.0), axis=1, keepdims=True)
        inflow = jnp.where(in_on, jnp.exp(col), 0.0)
        flow = jnp.dot(
            qact[:, cols], inc[h // owned, h % owned], preferred_element_type=F32
        )
        out = acc[:, cols] + flow * inflow
        acc[:, cols] = out
        sqsum[...] += out * out
        return carry

    lax.fori_loop(0, heads, carried, 0, unroll=2)

    def sq_copy(hp, source):
        return pltpu.make_async_remote_copy(
            src_ref=sqsum,
            dst_ref=sqgot.at[source],
            send_sem=s_send.at[hp],
            recv_sem=s_recv.at[source],
            device_id=(me, hp),
            device_id_type=MESH,
        )

    for hp in range(head_size):

        @pl.when(hp != hd)
        def _():
            sq_copy(hp, hd).start()

    sqgot[hd] = sqsum[...]
    for hp in range(head_size):

        @pl.when(hp != hd)
        def _():
            sq_copy(hp, hp).wait_recv()

    squares = sqgot[0]
    for hp in range(1, head_size):
        squares = squares + sqgot[hp]
    features = head_size * heads * D
    norm = lax.rsqrt(jnp.sum(squares, axis=1, keepdims=True) / features + NORM_EPS)

    def finish(h, carry):
        cols = head_cols(h)
        gate = sigmoid(lg[:, cols].astype(F32))
        lin_out[:, cols] = (acc[:, cols] * norm * gain[:, cols] * gate).astype(BF16)
        return carry

    lax.fori_loop(0, heads, finish, 0, unroll=2)

    for part in range(parts):

        @pl.when(z + 1 < planes)
        def _():
            wait_send(kv_up(part))

            @pl.when(z >= 1)
            def _():
                wait_send(kv_up_again(part))

        for p in range(PLANE):

            @pl.when(p > o)
            def _():
                wait_send(kv_own(part, p))

            @pl.when((p != o) & (z >= 1))
            def _():
                wait_send(kv_relay(part, 1, p))

            @pl.when((p < o) & (z >= 2))
            def _():
                wait_send(kv_relay(part, 2, p))

    for p in range(PLANE):

        @pl.when(p != o)
        def _():
            wait_send(fr_pair(p, o))
            in_copy(p, o).wait_send()

    @pl.when(z + 1 < planes)
    def _():
        ups[0].wait_send()
        ups[1].wait_send()

        @pl.when(z >= 1)
        def _():
            ups[2].wait_send()

    for hp in range(head_size):

        @pl.when(hp != hd)
        def _():
            sq_copy(hp, hd).wait_send()


def on_device(planes, head_size, lq, lk, lv, lg, ld, gain, sq, sk, sv, lens):
    rows, width = lq.shape
    heads = width // D
    owned = heads // PLANE
    kv_width = sk.shape[1]
    vmem = pl.BlockSpec(memory_space=pltpu.VMEM)
    dma = pltpu.SemaphoreType.DMA
    states = (owned, D, D)
    factors = (owned, 8, D)
    return pl.pallas_call(
        functools.partial(kernel, planes, head_size),
        out_shape=(
            jax.ShapeDtypeStruct((rows, width), BF16),
            jax.ShapeDtypeStruct((rows, width), BF16),
        ),
        in_specs=[vmem] * 9 + [pl.BlockSpec(memory_space=pltpu.SMEM)],
        out_specs=(vmem, vmem),
        scratch_shapes=[
            pltpu.VMEM((rows, width), BF16),
            pltpu.VMEM((rows, width), BF16),
            pltpu.VMEM((rows, width), BF16),
            pltpu.VMEM((rows, width), F32),
            pltpu.VMEM((REACH + 1, rows, kv_width), BF16),
            pltpu.VMEM((REACH + 1, rows, kv_width), BF16),
            pltpu.VMEM((PLANE,) + states, BF16),
            pltpu.VMEM((PLANE,) + factors, F32),
            pltpu.VMEM((PLANE,) + states, BF16),
            pltpu.VMEM((PLANE,) + factors, F32),
            pltpu.VMEM(states, BF16),
            pltpu.VMEM(factors, F32),
            pltpu.VMEM(states, BF16),
            pltpu.VMEM(states, BF16),
            pltpu.VMEM(factors, F32),
            pltpu.VMEM((PLANE,) + states, BF16),
            pltpu.VMEM((PLANE,) + states, BF16),
            pltpu.VMEM((heads, rows), F32),
            pltpu.VMEM((rows, rows), F32),
            pltpu.VMEM((rows, (REACH + 1) * rows), F32),
            pltpu.VMEM((rows, D), F32),
            pltpu.VMEM((head_size, rows, D), F32),
            dma((2, 4, 3 * PLANE + 2)),
            dma((2, 4, REACH + 1)),
            dma((2, PLANE)),
            dma((2, PLANE)),
            dma((3,)),
            dma((3,)),
            dma((PLANE,)),
            dma((PLANE,)),
            dma((head_size,)),
            dma((head_size,)),
        ],
        compiler_params=pltpu.CompilerParams(
            collective_id=0, has_side_effects=True, vmem_limit_bytes=56 << 20
        ),
    )(lq, lk, lv, lg, ld, gain.reshape(1, width), sq, sk, sv, lens)


def solution(mesh):
    tokens = P("seq", "head")
    body = functools.partial(on_device, mesh.shape["seq"] // PLANE, mesh.shape["head"])
    return jax.shard_map(
        body,
        mesh=mesh,
        in_specs=(tokens,) * 4 + (P("head", "seq"), P("head")) + (tokens,) * 3 + (P(),),
        out_specs=(tokens, tokens),
        check_vma=False,
    )
```
